32 devices in a mesh: ja: 8 (over z, y), pt: 4 (over x, core).
Axes of the slice: x: 2, y: 2, z: 4, core: 2. Of those that a mesh axis runs over, the one named last changes fastest.
Arguments:
- amplitudes: bfloat16 [8, 4, 3072, 512], P('ja', 'pt'), may hold values from -6 to 6
- live_rows: int32 [8, 4], P('ja', 'pt'), may hold values from 384 to 3072, as said below
- hole_coupling: bfloat16 [8, 4, 3, 512, 512], P('ja', 'pt'), may hold values from -0.25 to 0.25
- part_hole: bfloat16 [8, 4, 3072, 512], P('ja', 'pt'), may hold values from -0.0048828125 to 0.0048828125
- recoupling: float32 [8, 3], replicated, may hold values from -1 to 1
Outputs:
- operator_bar: bfloat16 [8, 4, 3072, 512], P('ja', 'pt')
The draws below stay inside these ranges and needn't reach their ends.
Inputs may be any that keep to these rules, and one draw needn't show every extreme that they name: `live_rows`: rows in use of a channel; some channel has exactly 3072.
All inputs are finite; a program needn't handle non-finite values.
Results may differ from the reference program's by a relative error of at most 0.0085.
Values may be sent and summed in bfloat16 or wider, within the bound.
A program may use at most 128 MiB of HBM per device.

```python
import jax
import jax.numpy as jnp
import numpy as np
from jax import lax

H = 512
P_SIZE = 3072
NJ = 8


def draw_live_rows(key, part):
    first_key, second_key = jax.random.split(jax.random.fold_in(key, 17))
    values = jax.random.randint(first_key, (NJ * 4,), P_SIZE // 8, P_SIZE + 1, dtype=jnp.int32)
    chosen = jax.random.randint(second_key, (), 0, NJ * 4, dtype=jnp.int32)
    values = jnp.where(jnp.arange(NJ * 4, dtype=jnp.int32) == chosen, P_SIZE, values)
    return values.reshape(NJ, 4).astype(jnp.int32)


def level_of(own_key, extent, shards, smallest, largest):
    def one(dim, parts):
        heights = jax.random.uniform(jax.random.fold_in(jax.random.fold_in(own_key, 6), dim), (parts,), jnp.float32, smallest / len(shards), largest / len(shards))
        return jnp.repeat(jnp.exp(heights), extent[dim] // parts).reshape((-1,) + (1,) * (len(extent) - dim - 1))

    loudness = one(*shards[0])
    for cut in shards[1:]:
        loudness = loudness * one(*cut)
    return loudness


def noise(key, dims, scale, limit, pieces=(), kind=jnp.bfloat16):
    loudness = level_of(key, dims, pieces, -0.22, 0.18) if pieces else 1.0
    values = jax.random.normal(key, dims, jnp.float32) * scale * loudness
    return jnp.minimum(jnp.maximum(values, -limit), limit).astype(kind)


def setup_inputs(seed: int = 0) -> dict:
    seeds = jax.random.split(jax.random.key(seed), 6)
    amplitudes = noise(seeds[0], (NJ, 4, P_SIZE, H), 1.0, 6.0, ((0, 8), (1, 4)))
    live_rows = draw_live_rows(jax.random.fold_in(seeds[5], 71), 0)
    hole_coupling = noise(seeds[2], (NJ, 4, 3, H, H), H ** -0.5, 0.25, ((0, 8), (1, 4)))
    part_hole = noise(seeds[3], (NJ, 4, P_SIZE, H), (P_SIZE * H) ** -0.5, 0.0048828125, ((0, 8), (1, 4)))
    recoupling = jnp.clip(jax.random.uniform(seeds[4], (NJ, 3), jnp.float32, -1.0, 1.0), -1.0, 1.0)
    return dict(amplitudes=amplitudes, live_rows=live_rows, hole_coupling=hole_coupling, part_hole=part_hole, recoupling=recoupling)


def segment_weights(recoupling):
    chan_total = recoupling.shape[0]
    half_count = chan_total // 2
    position = jnp.arange(chan_total, dtype=jnp.int32) % half_count
    keep = jnp.stack([position > 0, position >= 0, position < half_count - 1], axis=1)
    return jnp.where(keep, recoupling, jnp.zeros((), recoupling.dtype))


def reference(amplitudes, live_rows, hole_coupling, part_hole, recoupling):
    chan_total = amplitudes.shape[0]
    row_count = amplitudes.shape[2]
    hole_count = amplitudes.shape[3]
    partner = np.array([2, 3, 0, 1])
    row_ids = jnp.arange(row_count, dtype=jnp.int32)
    weights_all = segment_weights(recoupling)

    def masked(index):
        live_mask = row_ids[None, :] < live_rows[index][:, None]
        return jnp.where(live_mask[:, :, None], amplitudes[index], jnp.zeros((), amplitudes.dtype))

    def intermediate(index):
        return jnp.einsum("qph,qpk->qhk", masked(index).astype(jnp.float32),
                          part_hole[index].astype(jnp.float32)).astype(jnp.bfloat16)

    inter_hh = lax.map(intermediate, jnp.arange(chan_total, dtype=jnp.int32))

    def target(index):
        term_sum = jnp.zeros((4, row_count, hole_count), jnp.float32)
        mixing = jnp.zeros((4, hole_count, hole_count), jnp.float32)
        for offset in range(3):
            source_j = index + offset - 1
            valid = (source_j >= 0) & (source_j < chan_total)
            clipped = jnp.clip(source_j, 0, chan_total - 1).astype(jnp.int32)
            factor = jnp.where(valid, weights_all[clipped, 2 - offset], jnp.zeros((), recoupling.dtype))
            source = masked(clipped)[partner].astype(jnp.float32)
            hole_block = hole_coupling[clipped][partner][:, 2 - offset].astype(jnp.float32)
            term_sum = term_sum + factor * jnp.einsum("qph,qhk->qpk", source, hole_block)
            mixing = mixing + factor * inter_hh[clipped][partner].astype(jnp.float32)
        mix_bf = mixing.astype(jnp.bfloat16)
        own = masked(index)
        term_sum = term_sum + jnp.einsum("qph,qhk->qpk", own.astype(jnp.float32), mix_bf.astype(jnp.float32))
        live_mask = row_ids[None, :] < live_rows[index][:, None]
        return jnp.where(live_mask[:, :, None], term_sum, jnp.zeros((), term_sum.dtype)).astype(jnp.bfloat16)

    return lax.map(target, jnp.arange(chan_total, dtype=jnp.int32))
```

```python
import functools

import jax
import jax.numpy as jnp
from jax import lax
from jax.experimental import pallas as pl
from jax.experimental.pallas import tpu as pltpu
from jax.sharding import PartitionSpec as P

MESH = pl.DeviceIdType.MESH
CHUNK = 128
BLOCK = 512
HEAD = 4


def kernel(
    half, chunk, block, head,
    wts, live, amp_hbm, hole_hbm, part_hbm, out_hbm,
    amp, hole, part, acc, inter,
    far_out, far_in, near_out, near_in, side_out, side_in, result,
    amp_sem, part_sem, hole_sem,
    far_s, far_r, near_s, near_r, side_s, side_r, out_s,
):
    rows, holes = amp.shape
    terms = rows // chunk
    mixes = holes // chunk
    total = terms + mixes
    blocks = rows // block

    chan = lax.axis_index("ja")
    label = lax.axis_index("pt")
    pos = lax.rem(chan, half)
    base = chan - pos
    odd = lax.rem(chan, 2)
    near = chan + 1 - 2 * odd
    far_to = base + lax.rem(pos + half - 2 + 4 * odd, half)
    far_from = base + lax.rem(pos + half + 2 - 4 * odd, half)
    side = label + 2 - 4 * lax.rem(lax.div(label, 2), 2)

    def amp_copy(b):
        part_rows = pl.ds(pl.multiple_of(b * block, block), block)
        return pltpu.make_async_copy(amp_hbm.at[0, 0, part_rows], amp.at[part_rows], amp_sem.at[b])

    def part_copy(b):
        part_rows = pl.ds(pl.multiple_of(b * block, block), block)
        return pltpu.make_async_copy(part_hbm.at[0, 0, part_rows], part.at[part_rows], part_sem.at[b])

    hole_copy = pltpu.make_async_copy(hole_hbm.at[0, 0], hole, hole_sem)
    amp_copy(0).start()
    hole_copy.start()
    for b in range(blocks):
        if b:
            amp_copy(b).start()
        part_copy(b).start()

    barrier = pltpu.get_barrier_semaphore()
    targets = [{"ja": near}, {"pt": side}, {"ja": far_to}]
    if half != 4:
        targets.append({"ja": far_from})
    for target in targets:
        pl.semaphore_signal(barrier, inc=1, device_id=target, device_id_type=MESH)

    down = jnp.where(pos > 0, wts[chan, 0], 0.0)
    up = jnp.where(pos < half - 1, wts[chan, 2], 0.0)
    own_w = wts[chan, 1]
    near_slot = 2 - 2 * odd
    far_slot = 2 * odd
    near_w = jnp.where(odd == 0, up, down)
    far_w = jnp.where(odd == 0, down, up)
    live_count = live[0, 0]

    def at(k):
        return pl.ds(pl.multiple_of(k * chunk, chunk), chunk)

    def alive(first, count):
        ids = lax.broadcasted_iota(jnp.int32, (count, holes), 0) + first
        return ids < live_count

    def masked(first, count):
        vals = amp[pl.ds(pl.multiple_of(first, count), count)]
        return jnp.where(alive(first, count), vals, jnp.zeros_like(vals))

    def product(j, slot):
        return jnp.dot(masked(j * chunk, chunk), hole[slot], preferred_element_type=jnp.float32)

    def far_copy(k):
        return pltpu.make_async_remote_copy(
            src_ref=far_out.at[at(k)], dst_ref=far_in.at[at(k)],
            send_sem=far_s.at[k], recv_sem=far_r.at[k],
            device_id={"ja": far_to}, device_id_type=MESH,
        )

    def near_copy(k):
        return pltpu.make_async_remote_copy(
            src_ref=near_out.at[at(k)], dst_ref=near_in.at[at(k)],
            send_sem=near_s.at[k], recv_sem=near_r.at[k],
            device_id={"ja": near}, device_id_type=MESH,
        )

    def side_copy(k):
        return pltpu.make_async_remote_copy(
            src_ref=side_out.at[at(k)], dst_ref=side_in.at[at(k)],
            send_sem=side_s.at[k], recv_sem=side_r.at[k],
            device_id={"pt": side}, device_id_type=MESH,
        )

    def out_copy(j):
        return pltpu.make_async_copy(result.at[at(j)], out_hbm.at[0, 0, at(j)], out_s.at[j])

    def is_mix(k):
        return jnp.logical_and(k >= head, k < head + mixes)

    def fill(k, slot, weight, dst, src):
        def put(value):
            value = weight * value
            if src is not None:
                value = value + src[at(k)].astype(jnp.float32)
            dst[at(k)] = value.astype(jnp.bfloat16)

        @pl.when(is_mix(k))
        def _():
            put(inter[at(jnp.clip(k - head, 0, mixes - 1))].astype(jnp.float32))

        @pl.when(jnp.logical_not(is_mix(k)))
        def _():
            put(product(jnp.where(k < head, k, jnp.maximum(k - mixes, 0)), slot))

    amp_copy(0).wait()
    hole_copy.wait()
    pl.semaphore_wait(barrier, len(targets))

    @pl.loop(0, head)
    def _(k):
        far_out[at(k)] = (far_w * product(k, far_slot)).astype(jnp.bfloat16)
        far_copy(k).start()

    acc[...] = jnp.zeros_like(acc)

    @pl.loop(0, blocks)
    def _(b):
        @pl.when(b > 0)
        def _():
            amp_copy(b).wait()

        part_copy(b).wait()
        first = b * block
        acc[...] += lax.dot_general(
            masked(first, block), part[pl.ds(pl.multiple_of(first, block), block)],
            (((0,), (0,)), ((), ())), preferred_element_type=jnp.float32,
        )

    inter[...] = acc[...].astype(jnp.bfloat16)

    @pl.loop(head, head + mixes)
    def _(k):
        vals = inter[at(k - head)].astype(jnp.float32)
        far_out[at(k)] = (far_w * vals).astype(jnp.bfloat16)
        far_copy(k).start()

    lead = head + mixes
    lag = lead + 2

    @pl.loop(0, lag + terms)
    def _(t):
        @pl.when(t + lead < total)
        def _():
            k = t + lead
            far_out[at(k)] = (far_w * product(k - mixes, far_slot)).astype(jnp.bfloat16)
            far_copy(k).start()

        @pl.when(t < total)
        def _():
            far_copy(t).wait_recv()
            fill(t, near_slot, near_w, near_out, far_in)
            near_copy(t).start()

        @pl.when(jnp.logical_and(t >= 1, t < total + 1))
        def _():
            k = t - 1
            near_copy(k).wait_recv()
            fill(k, 1, own_w, side_out, near_in)
            side_copy(k).start()

        @pl.when(t == lag)
        def _():
            for m in range(mixes):
                side_copy(head + m).wait_recv()

        @pl.when(t >= lag)
        def _():
            j = t - lag
            k = jnp.where(j < head, j, j + mixes)
            side_copy(k).wait_recv()
            mix = side_in[head * chunk : head * chunk + holes]
            value = side_in[at(k)].astype(jnp.float32) + jnp.dot(
                masked(j * chunk, chunk), mix, preferred_element_type=jnp.float32
            )
            value = jnp.where(alive(j * chunk, chunk), value, jnp.zeros_like(value))
            result[at(j)] = value.astype(jnp.bfloat16)
            out_copy(j).start()

    @pl.loop(0, total)
    def _(k):
        far_copy(k).wait_send()
        near_copy(k).wait_send()
        side_copy(k).wait_send()

    @pl.loop(0, terms)
    def _(j):
        out_copy(j).wait()


def shards(half, amplitudes, live_rows, hole_coupling, part_hole, recoupling):
    rows, holes = amplitudes.shape[2:]
    chunk, block = min(CHUNK, holes), min(BLOCK, rows)
    total = (rows + holes) // chunk
    terms = rows // chunk
    bf = jnp.bfloat16
    stream = pltpu.VMEM((rows + holes, holes), bf)
    sems = pltpu.SemaphoreType.DMA
    flops = 10 * rows * holes * holes
    return pl.pallas_call(
        functools.partial(kernel, half, chunk, block, min(HEAD, terms)),
        out_shape=jax.ShapeDtypeStruct(amplitudes.shape, bf),
        in_specs=[pl.BlockSpec(memory_space=pltpu.SMEM)] * 2
        + [pl.BlockSpec(memory_space=pl.ANY)] * 3,
        out_specs=pl.BlockSpec(memory_space=pl.ANY),
        scratch_shapes=[
            pltpu.VMEM((rows, holes), bf),
            pltpu.VMEM((3, holes, holes), bf),
            pltpu.VMEM((rows, holes), bf),
            pltpu.VMEM((holes, holes), jnp.float32),
            pltpu.VMEM((holes, holes), bf),
            stream, stream, stream, stream, stream, stream,
            pltpu.VMEM((rows, holes), bf),
            sems((rows // block,)),
            sems((rows // block,)),
            sems,
            sems((total,)), sems((total,)), sems((total,)),
            sems((total,)), sems((total,)), sems((total,)),
            sems((terms,)),
        ],
        compiler_params=pltpu.CompilerParams(
            collective_id=0, has_side_effects=True, vmem_limit_bytes=56 << 20
        ),
        cost_estimate=pl.CostEstimate(
            flops=flops, bytes_accessed=6 * rows * holes * 2, transcendentals=0
        ),
        name="gt_bar",
    )(recoupling, live_rows, amplitudes, hole_coupling, part_hole)


def solution(mesh):
    in_specs = (
        P("ja", "pt", None, None),
        P("ja", "pt"),
        P("ja", "pt", None, None, None),
        P("ja", "pt", None, None),
        P(),
    )
    out_specs = P("ja", "pt", None, None)
    body = functools.partial(shards, mesh.shape["ja"] // 2)
    return jax.shard_map(body, mesh=mesh, in_specs=in_specs, out_specs=out_specs, check_vma=False)
```

```python
import functools

import jax
import jax.numpy as jnp
from jax import lax
from jax.experimental import pallas as pl
from jax.experimental.pallas import tpu as pltpu
from jax.sharding import PartitionSpec as P

MESH = pl.DeviceIdType.MESH
CHUNK = 128
BLOCK = 512
HEAD = 4
GAP = 1


def kernel(
    half, chunk, block, head,
    wts, live, amp_hbm, hole_hbm, part_hbm, out,
    amp, hole, part, acc, inter,
    far_out, far_in, near_out, near_in, side_out, side_in, near_p, side_p,
    amp_sem, part_sem, hole_sem,
    far_s, far_r, near_s, near_r, side_s, side_r,
):
    rows, holes = amp.shape
    terms = rows // chunk
    mixes = holes // chunk
    total = terms + mixes
    blocks = rows // block

    chan = lax.axis_index("ja")
    label = lax.axis_index("pt")
    pos = lax.rem(chan, half)
    base = chan - pos
    odd = lax.rem(chan, 2)
    near = chan + 1 - 2 * odd
    far_to = base + lax.rem(pos + half - 2 + 4 * odd, half)
    far_from = base + lax.rem(pos + half + 2 - 4 * odd, half)
    side = label + 2 - 4 * lax.rem(lax.div(label, 2), 2)

    def amp_copy(b):
        part_rows = pl.ds(pl.multiple_of(b * block, block), block)
        return pltpu.make_async_copy(amp_hbm.at[0, 0, part_rows], amp.at[part_rows], amp_sem.at[b])

    def part_copy(b):
        part_rows = pl.ds(pl.multiple_of(b * block, block), block)
        return pltpu.make_async_copy(part_hbm.at[0, 0, part_rows], part.at[part_rows], part_sem.at[b])

    hole_copy = pltpu.make_async_copy(hole_hbm.at[0, 0], hole, hole_sem)
    amp_copy(0).start()
    hole_copy.start()
    for b in range(blocks):
        if b:
            amp_copy(b).start()
        part_copy(b).start()

    barrier = pltpu.get_barrier_semaphore()
    targets = [{"ja": near}, {"pt": side}, {"ja": far_to}]
    if half != 4:
        targets.append({"ja": far_from})
    for target in targets:
        pl.semaphore_signal(barrier, inc=1, device_id=target, device_id_type=MESH)

    down = jnp.where(pos > 0, wts[0, chan], 0.0)
    up = jnp.where(pos < half - 1, wts[2, chan], 0.0)
    own_w = wts[1, chan]
    near_slot = 2 - 2 * odd
    far_slot = 2 * odd
    near_w = jnp.where(odd == 0, up, down)
    far_w = jnp.where(odd == 0, down, up)
    live_count = live[0, 0]

    def at(k):
        return pl.ds(pl.multiple_of(k * chunk, chunk), chunk)

    def alive(first, count):
        ids = lax.broadcasted_iota(jnp.int32, (count, holes), 0) + first
        return ids < live_count

    def masked(first, count):
        vals = amp[pl.ds(pl.multiple_of(first, count), count)]
        return jnp.where(alive(first, count), vals, jnp.zeros_like(vals))

    def product(j, slot):
        return jnp.dot(masked(j * chunk, chunk), hole[slot], preferred_element_type=jnp.float32)

    def far_copy(k):
        return pltpu.make_async_remote_copy(
            src_ref=far_out.at[at(k)], dst_ref=far_in.at[at(k)],
            send_sem=far_s.at[k], recv_sem=far_r.at[k],
            device_id={"ja": far_to}, device_id_type=MESH,
        )

    def near_copy(k):
        return pltpu.make_async_remote_copy(
            src_ref=near_out.at[at(k)], dst_ref=near_in.at[at(k)],
            send_sem=near_s.at[k], recv_sem=near_r.at[k],
            device_id={"ja": near}, device_id_type=MESH,
        )

    def side_copy(k):
        return pltpu.make_async_remote_copy(
            src_ref=side_out.at[at(k)], dst_ref=side_in.at[at(k)],
            send_sem=side_s.at[k], recv_sem=side_r.at[k],
            device_id={"pt": side}, device_id_type=MESH,
        )

    def is_mix(k):
        return jnp.logical_and(k >= head, k < head + mixes)

    def own(k, slot, weight, dst):
        @pl.when(is_mix(k))
        def _():
            dst[...] = weight * inter[at(jnp.clip(k - head, 0, mixes - 1))].astype(jnp.float32)

        @pl.when(jnp.logical_not(is_mix(k)))
        def _():
            dst[...] = weight * product(jnp.where(k < head, k, jnp.maximum(k - mixes, 0)), slot)

    def add(k, ready, src, dst):
        dst[at(k)] = (ready[...] + src[at(k)].astype(jnp.float32)).astype(jnp.bfloat16)

    amp_copy(0).wait()
    hole_copy.wait()
    pl.semaphore_wait(barrier, len(targets))

    @pl.loop(0, head)
    def _(k):
        far_out[at(k)] = (far_w * product(k, far_slot)).astype(jnp.bfloat16)
        far_copy(k).start()

    acc[...] = jnp.zeros_like(acc)

    @pl.loop(0, blocks)
    def _(b):
        @pl.when(b > 0)
        def _():
            amp_copy(b).wait()

        part_copy(b).wait()
        first = b * block
        acc[...] += lax.dot_general(
            masked(first, block), part[pl.ds(pl.multiple_of(first, block), block)],
            (((0,), (0,)), ((), ())), preferred_element_type=jnp.float32,
        )

    inter[...] = acc[...].astype(jnp.bfloat16)

    @pl.loop(head, head + mixes)
    def _(k):
        vals = inter[at(k - head)].astype(jnp.float32)
        far_out[at(k)] = (far_w * vals).astype(jnp.bfloat16)
        far_copy(k).start()

    lead = head + mixes
    lag = lead + GAP + 2

    @pl.loop(0, lag + terms)
    def _(t):
        @pl.when(t + lead < total)
        def _():
            k = t + lead
            far_out[at(k)] = (far_w * product(k - mixes, far_slot)).astype(jnp.bfloat16)
            far_copy(k).start()

        @pl.when(t < total)
        def _():
            own(t, near_slot, near_w, near_p)

        @pl.when(jnp.logical_and(t >= GAP, t < total + GAP))
        def _():
            own(t - GAP, 1, own_w, side_p)

        @pl.when(t < total)
        def _():
            far_copy(t).wait_recv()
            add(t, near_p, far_in, near_out)
            near_copy(t).start()

        @pl.when(jnp.logical_and(t >= GAP, t < total + GAP))
        def _():
            k = t - GAP
            near_copy(k).wait_recv()
            add(k, side_p, near_in, side_out)
            side_copy(k).start()

        @pl.when(t == lag)
        def _():
            for m in range(mixes):
                side_copy(head + m).wait_recv()

        @pl.when(t >= lag)
        def _():
            j = t - lag
            k = jnp.where(j < head, j, j + mixes)
            side_copy(k).wait_recv()
            mix = side_in[head * chunk : head * chunk + holes]
            value = side_in[at(k)].astype(jnp.float32) + jnp.dot(
                masked(j * chunk, chunk), mix, preferred_element_type=jnp.float32
            )
            value = jnp.where(alive(j * chunk, chunk), value, jnp.zeros_like(value))
            out[0, 0, at(j)] = value.astype(jnp.bfloat16)

    @pl.loop(0, total)
    def _(k):
        far_copy(k).wait_send()
        near_copy(k).wait_send()
        side_copy(k).wait_send()


def shards(half, amplitudes, live_rows, hole_coupling, part_hole, recoupling):
    rows, holes = amplitudes.shape[2:]
    chunk, block = min(CHUNK, holes), min(BLOCK, rows)
    total = (rows + holes) // chunk
    terms = rows // chunk
    bf = jnp.bfloat16
    stream = pltpu.VMEM((rows + holes, holes), bf)
    sems = pltpu.SemaphoreType.DMA
    flops = 10 * rows * holes * holes
    return pl.pallas_call(
        functools.partial(kernel, half, chunk, block, min(HEAD, terms)),
        out_shape=pltpu.VMEM(amplitudes.shape, bf),
        in_specs=[pl.BlockSpec(memory_space=pltpu.SMEM)] * 2
        + [pl.BlockSpec(memory_space=pl.ANY)] * 3,
        out_specs=pl.BlockSpec(memory_space=pltpu.VMEM),
        scratch_shapes=[
            pltpu.VMEM((rows, holes), bf),
            pltpu.VMEM((3, holes, holes), bf),
            pltpu.VMEM((rows, holes), bf),
            pltpu.VMEM((holes, holes), jnp.float32),
            pltpu.VMEM((holes, holes), bf),
            stream, stream, stream, stream, stream, stream,
            pltpu.VMEM((chunk, holes), jnp.float32),
            pltpu.VMEM((chunk, holes), jnp.float32),
            sems((rows // block,)),
            sems((rows // block,)),
            sems,
            sems((total,)), sems((total,)), sems((total,)),
            sems((total,)), sems((total,)), sems((total,)),
        ],
        compiler_params=pltpu.CompilerParams(
            collective_id=0, has_side_effects=True, vmem_limit_bytes=60 << 20
        ),
        cost_estimate=pl.CostEstimate(
            flops=flops, bytes_accessed=6 * rows * holes * 2, transcendentals=0
        ),
        name="gt_bar",
    )(recoupling.T, live_rows, amplitudes, hole_coupling, part_hole)


def solution(mesh):
    in_specs = (
        P("ja", "pt", None, None),
        P("ja", "pt"),
        P("ja", "pt", None, None, None),
        P("ja", "pt", None, None),
        P(),
    )
    out_specs = P("ja", "pt", None, None)
    body = functools.partial(shards, mesh.shape["ja"] // 2)
    return jax.shard_map(body, mesh=mesh, in_specs=in_specs, out_specs=out_specs, check_vma=False)
```

```python
import functools

import jax
import jax.numpy as jnp
from jax import lax
from jax.experimental import pallas as pl
from jax.experimental.pallas import tpu as pltpu
from jax.sharding import PartitionSpec as P

MESH = pl.DeviceIdType.MESH
CHUNK = 128
BLOCK = 512
HEAD = 4
GAP = 2


def kernel(
    half, chunk, block, head,
    wts, live, amp_hbm, hole_hbm, part_hbm, out,
    amp, hole, part, acc, inter, mix_in, mix, early,
    far_out, far_in, near_out, near_in, side_out, side_in, near_p, side_p,
    amp_sem, part_sem, hole_sem,
    far_s, far_r, near_s, near_r, side_s, side_r, mix_s, mix_r,
):
    rows, holes = amp.shape
    terms = rows // chunk
    mixes = holes // chunk
    total = terms + mixes
    blocks = rows // block
    split = holes - chunk

    chan = lax.axis_index("ja")
    label = lax.axis_index("pt")
    pos = lax.rem(chan, half)
    base = chan - pos
    odd = lax.rem(chan, 2)
    near = chan + 1 - 2 * odd
    far_to = base + lax.rem(pos + half - 2 + 4 * odd, half)
    far_from = base + lax.rem(pos + half + 2 - 4 * odd, half)
    side = label + 2 - 4 * lax.rem(lax.div(label, 2), 2)

    def amp_copy(b):
        part_rows = pl.ds(pl.multiple_of(b * block, block), block)
        return pltpu.make_async_copy(amp_hbm.at[0, 0, part_rows], amp.at[part_rows], amp_sem.at[b])

    def part_copy(b):
        part_rows = pl.ds(pl.multiple_of(b * block, block), block)
        return pltpu.make_async_copy(part_hbm.at[0, 0, part_rows], part.at[part_rows], part_sem.at[b])

    def hole_copy(slot):
        return pltpu.make_async_copy(hole_hbm.at[0, 0, slot], hole.at[slot], hole_sem.at[slot])

    near_slot = 2 - 2 * odd
    far_slot = 2 * odd
    amp_copy(0).start()
    hole_copy(far_slot).start()
    for b in range(blocks):
        if b:
            amp_copy(b).start()
        part_copy(b).start()
    hole_copy(near_slot).start()
    hole_copy(1).start()

    barrier = pltpu.get_barrier_semaphore()
    targets = [{"ja": near}, {"pt": side}, {"ja": far_to}]
    if half != 4:
        targets.append({"ja": far_from})
    for target in targets:
        pl.semaphore_signal(barrier, inc=1, device_id=target, device_id_type=MESH)

    down = jnp.where(pos > 0, wts[0, chan], 0.0)
    up = jnp.where(pos < half - 1, wts[2, chan], 0.0)
    own_w = wts[1, chan]
    near_w = jnp.where(odd == 0, up, down)
    far_w = jnp.where(odd == 0, down, up)
    live_count = live[0, 0]

    def at(k):
        return pl.ds(pl.multiple_of(k * chunk, chunk), chunk)

    def alive(first, count):
        ids = lax.broadcasted_iota(jnp.int32, (count, holes), 0) + first
        return ids < live_count

    def masked(first, count):
        vals = amp[pl.ds(pl.multiple_of(first, count), count)]
        return jnp.where(alive(first, count), vals, jnp.zeros_like(vals))

    def product(j, slot):
        return jnp.dot(masked(j * chunk, chunk), hole[slot], preferred_element_type=jnp.float32)

    def far_copy(k):
        return pltpu.make_async_remote_copy(
            src_ref=far_out.at[at(k)], dst_ref=far_in.at[at(k)],
            send_sem=far_s.at[k], recv_sem=far_r.at[k],
            device_id={"ja": far_to}, device_id_type=MESH,
        )

    def near_copy(k):
        return pltpu.make_async_remote_copy(
            src_ref=near_out.at[at(k)], dst_ref=near_in.at[at(k)],
            send_sem=near_s.at[k], recv_sem=near_r.at[k],
            device_id={"ja": near}, device_id_type=MESH,
        )

    def side_copy(k):
        return pltpu.make_async_remote_copy(
            src_ref=side_out.at[at(k)], dst_ref=side_in.at[at(k)],
            send_sem=side_s.at[k], recv_sem=side_r.at[k],
            device_id={"pt": side}, device_id_type=MESH,
        )

    def mix_copy(m):
        return pltpu.make_async_remote_copy(
            src_ref=inter.at[at(m)], dst_ref=mix_in.at[at(m)],
            send_sem=mix_s.at[m], recv_sem=mix_r.at[m],
            device_id={"pt": side}, device_id_type=MESH,
        )

    def own(k, slot, weight, put):
        @pl.when(k >= terms)
        def _():
            put(weight * mix_in[at(jnp.maximum(k - terms, 0))].astype(jnp.float32))

        @pl.when(k < terms)
        def _():
            put(weight * product(jnp.minimum(k, terms - 1), slot))

    def send_far(k):
        def put(value):
            far_out[at(k)] = value.astype(jnp.bfloat16)

        own(k, far_slot, far_w, put)
        far_copy(k).start()

    def put_near(value):
        near_p[...] = value

    def put_side(value):
        side_p[...] = value

    amp_copy(0).wait()
    hole_copy(far_slot).wait()
    pl.semaphore_wait(barrier, len(targets))

    @pl.loop(0, head)
    def _(k):
        far_out[at(k)] = (far_w * product(k, far_slot)).astype(jnp.bfloat16)
        far_copy(k).start()

    acc[...] = jnp.zeros_like(acc)

    @pl.loop(0, blocks)
    def _(b):
        @pl.when(b > 0)
        def _():
            amp_copy(b).wait()

        part_copy(b).wait()
        first = b * block
        acc[...] += lax.dot_general(
            masked(first, block), part[pl.ds(pl.multiple_of(first, block), block)],
            (((0,), (0,)), ((), ())), preferred_element_type=jnp.float32,
        )

    inter[...] = acc[...].astype(jnp.bfloat16)

    @pl.loop(0, mixes)
    def _(m):
        mix_copy(m).start()

    hole_copy(near_slot).wait()
    hole_copy(1).wait()

    @pl.loop(0, total + GAP)
    def _(t):
        @pl.when(t + head == terms)
        def _():
            for m in range(mixes):
                mix_copy(m).wait_recv()

        @pl.when(t + head < total)
        def _():
            send_far(t + head)

        @pl.when(t < total)
        def _():
            own(t, near_slot, near_w, put_near)

        @pl.when(t >= GAP)
        def _():
            own(jnp.maximum(t - GAP, 0), 1, own_w, put_side)

        @pl.when(t < total)
        def _():
            far_copy(t).wait_recv()
            value = near_p[...] + far_in[at(t)].astype(jnp.float32)
            near_out[at(t)] = value.astype(jnp.bfloat16)
            near_copy(t).start()

        @pl.when(t >= GAP)
        def _():
            k = jnp.maximum(t - GAP, 0)
            near_copy(k).wait_recv()
            value = (side_p[...] + near_in[at(k)].astype(jnp.float32)).astype(jnp.bfloat16)

            @pl.when(k < terms)
            def _():
                j = jnp.minimum(k, terms - 1)
                side_out[at(j)] = value
                side_copy(j).start()

            @pl.when(k >= terms)
            def _():
                mix[at(jnp.maximum(k - terms, 0))] = value

        @pl.when(t == total + GAP - 2)
        def _():
            @pl.loop(0, blocks)
            def _(b):
                where = pl.ds(pl.multiple_of(b * block, block), block)
                early[where] = jnp.dot(
                    amp[where, :split], mix[:split], preferred_element_type=jnp.float32
                )

    @pl.loop(0, blocks)
    def _(b):
        for c in range(block // chunk):
            side_copy(b * (block // chunk) + c).wait_recv()
        where = pl.ds(pl.multiple_of(b * block, block), block)
        value = early[where] + side_in[where].astype(jnp.float32)
        value = value + jnp.dot(
            amp[where, split:], mix[split:], preferred_element_type=jnp.float32
        )
        value = jnp.where(alive(b * block, block), value, jnp.zeros_like(value))
        out[0, 0, where] = value.astype(jnp.bfloat16)

    @pl.loop(0, total)
    def _(k):
        far_copy(k).wait_send()
        near_copy(k).wait_send()

    @pl.loop(0, terms)
    def _(k):
        side_copy(k).wait_send()

    @pl.loop(0, mixes)
    def _(m):
        mix_copy(m).wait_send()


def shards(half, amplitudes, live_rows, hole_coupling, part_hole, recoupling):
    rows, holes = amplitudes.shape[2:]
    chunk, block = min(CHUNK, holes), min(BLOCK, rows)
    total = (rows + holes) // chunk
    terms = rows // chunk
    bf = jnp.bfloat16
    stream = pltpu.VMEM((rows + holes, holes), bf)
    sems = pltpu.SemaphoreType.DMA
    flops = 10 * rows * holes * holes
    return pl.pallas_call(
        functools.partial(kernel, half, chunk, block, min(HEAD, block // chunk)),
        out_shape=pltpu.VMEM(amplitudes.shape, bf),
        in_specs=[pl.BlockSpec(memory_space=pltpu.SMEM)] * 2
        + [pl.BlockSpec(memory_space=pl.ANY)] * 3,
        out_specs=pl.BlockSpec(memory_space=pltpu.VMEM),
        scratch_shapes=[
            pltpu.VMEM((rows, holes), bf),
            pltpu.VMEM((3, holes, holes), bf),
            pltpu.VMEM((rows, holes), bf),
            pltpu.VMEM((holes, holes), jnp.float32),
            pltpu.VMEM((holes, holes), bf),
            pltpu.VMEM((holes, holes), bf),
            pltpu.VMEM((holes, holes), bf),
            pltpu.VMEM((rows, holes), jnp.float32),
            stream, stream, stream, stream,
            pltpu.VMEM((rows, holes), bf),
            pltpu.VMEM((rows, holes), bf),
            pltpu.VMEM((chunk, holes), jnp.float32),
            pltpu.VMEM((chunk, holes), jnp.float32),
            sems((rows // block,)),
            sems((rows // block,)),
            sems((3,)),
            sems((total,)), sems((total,)), sems((total,)), sems((total,)),
            sems((terms,)), sems((terms,)),
            sems((holes // chunk,)), sems((holes // chunk,)),
        ],
        compiler_params=pltpu.CompilerParams(
            collective_id=0, has_side_effects=True, vmem_limit_bytes=60 << 20
        ),
        cost_estimate=pl.CostEstimate(
            flops=flops, bytes_accessed=6 * rows * holes * 2, transcendentals=0
        ),
        name="gt_bar",
    )(recoupling.T, live_rows, amplitudes, hole_coupling, part_hole)


def solution(mesh):
    in_specs = (
        P("ja", "pt", None, None),
        P("ja", "pt"),
        P("ja", "pt", None, None, None),
        P("ja", "pt", None, None),
        P(),
    )
    out_specs = P("ja", "pt", None, None)
    body = functools.partial(shards, mesh.shape["ja"] // 2)
    return jax.shard_map(body, mesh=mesh, in_specs=in_specs, out_specs=out_specs, check_vma=False)
```

```python
import functools

import jax
import jax.numpy as jnp
from jax import lax
from jax.experimental import pallas as pl
from jax.experimental.pallas import tpu as pltpu
from jax.sharding import PartitionSpec as P

MESH = pl.DeviceIdType.MESH
CHUNK = 128
BLOCK = 512
HEAD = 4
GAP = 3


def kernel(
    half, chunk, block, head,
    wts, live, amp_hbm, hole_hbm, part_hbm, out,
    amp, hole, part, acc, inter, mix_in, mix, early,
    far_out, far_in, near_out, near_in, side_out, side_in, near_p, side_p,
    amp_sem, part_sem, hole_sem,
    far_s, far_r, near_s, near_r, side_s, side_r, mix_s, mix_r,
):
    rows, holes = amp.shape
    terms = rows // chunk
    mixes = holes // chunk
    total = terms + mixes
    blocks = rows // block
    split = holes - chunk

    chan = lax.axis_index("ja")
    label = lax.axis_index("pt")
    pos = lax.rem(chan, half)
    base = chan - pos
    odd = lax.rem(chan, 2)
    near = chan + 1 - 2 * odd
    far_to = base + lax.rem(pos + half - 2 + 4 * odd, half)
    far_from = base + lax.rem(pos + half + 2 - 4 * odd, half)
    side = label + 2 - 4 * lax.rem(lax.div(label, 2), 2)

    def amp_copy(b):
        part_rows = pl.ds(pl.multiple_of(b * block, block), block)
        return pltpu.make_async_copy(amp_hbm.at[0, 0, part_rows], amp.at[part_rows], amp_sem.at[b])

    def part_copy(b):
        part_rows = pl.ds(pl.multiple_of(b * block, block), block)
        return pltpu.make_async_copy(part_hbm.at[0, 0, part_rows], part.at[part_rows], part_sem.at[b])

    def hole_copy(slot):
        return pltpu.make_async_copy(hole_hbm.at[0, 0, slot], hole.at[slot], hole_sem.at[slot])

    near_slot = 2 - 2 * odd
    far_slot = 2 * odd
    amp_copy(0).start()
    hole_copy(far_slot).start()
    for b in range(blocks):
        if b:
            amp_copy(b).start()
        part_copy(b).start()
    hole_copy(near_slot).start()
    hole_copy(1).start()

    barrier = pltpu.get_barrier_semaphore()
    targets = [{"ja": near}, {"pt": side}, {"ja": far_to}]
    if half != 4:
        targets.append({"ja": far_from})
    for target in targets:
        pl.semaphore_signal(barrier, inc=1, device_id=target, device_id_type=MESH)

    down = jnp.where(pos > 0, wts[0, chan], 0.0)
    up = jnp.where(pos < half - 1, wts[2, chan], 0.0)
    own_w = wts[1, chan]
    near_w = jnp.where(odd == 0, up, down)
    far_w = jnp.where(odd == 0, down, up)
    live_count = live[0, 0]

    def at(k):
        return pl.ds(pl.multiple_of(k * chunk, chunk), chunk)

    def alive(first, count):
        ids = lax.broadcasted_iota(jnp.int32, (count, holes), 0) + first
        return ids < live_count

    def masked(first, count):
        vals = amp[pl.ds(pl.multiple_of(first, count), count)]
        return jnp.where(alive(first, count), vals, jnp.zeros_like(vals))

    def product(j, slot):
        return jnp.dot(masked(j * chunk, chunk), hole[slot], preferred_element_type=jnp.float32)

    def far_copy(k):
        return pltpu.make_async_remote_copy(
            src_ref=far_out.at[at(k)], dst_ref=far_in.at[at(k)],
            send_sem=far_s.at[k], recv_sem=far_r.at[k],
            device_id={"ja": far_to}, device_id_type=MESH,
        )

    def near_copy(k):
        return pltpu.make_async_remote_copy(
            src_ref=near_out.at[at(k)], dst_ref=near_in.at[at(k)],
            send_sem=near_s.at[k], recv_sem=near_r.at[k],
            device_id={"ja": near}, device_id_type=MESH,
        )

    def side_copy(k):
        return pltpu.make_async_remote_copy(
            src_ref=side_out.at[at(k)], dst_ref=side_in.at[at(k)],
            send_sem=side_s.at[k], recv_sem=side_r.at[k],
            device_id={"pt": side}, device_id_type=MESH,
        )

    def mix_copy(m):
        return pltpu.make_async_remote_copy(
            src_ref=inter.at[at(m)], dst_ref=mix_in.at[at(m)],
            send_sem=mix_s.at[m], recv_sem=mix_r.at[m],
            device_id={"pt": side}, device_id_type=MESH,
        )

    def own(k, slot, weight, put):
        @pl.when(k >= terms)
        def _():
            put(weight * mix_in[at(jnp.maximum(k - terms, 0))].astype(jnp.float32))

        @pl.when(k < terms)
        def _():
            put(weight * product(jnp.minimum(k, terms - 1), slot))

    def send_far(k):
        def put(value):
            far_out[at(k)] = value.astype(jnp.bfloat16)

        own(k, far_slot, far_w, put)
        far_copy(k).start()

    def put_near(value):
        near_p[...] = value

    def put_side(value):
        side_p[...] = value

    amp_copy(0).wait()
    hole_copy(far_slot).wait()
    pl.semaphore_wait(barrier, len(targets))

    @pl.loop(0, head)
    def _(k):
        far_out[at(k)] = (far_w * product(k, far_slot)).astype(jnp.bfloat16)
        far_copy(k).start()

    acc[...] = jnp.zeros_like(acc)

    @pl.loop(0, blocks)
    def _(b):
        @pl.when(b > 0)
        def _():
            amp_copy(b).wait()

        part_copy(b).wait()
        first = b * block
        acc[...] += lax.dot_general(
            masked(first, block), part[pl.ds(pl.multiple_of(first, block), block)],
            (((0,), (0,)), ((), ())), preferred_element_type=jnp.float32,
        )

    inter[...] = acc[...].astype(jnp.bfloat16)

    @pl.loop(0, mixes)
    def _(m):
        mix_copy(m).start()

    hole_copy(near_slot).wait()
    hole_copy(1).wait()

    @pl.loop(0, total + GAP)
    def _(t):
        @pl.when(t + head == terms)
        def _():
            for m in range(mixes):
                mix_copy(m).wait_recv()

        @pl.when(t + head < total)
        def _():
            send_far(t + head)

        @pl.when(t < total)
        def _():
            own(t, near_slot, near_w, put_near)

        @pl.when(t >= GAP)
        def _():
            own(jnp.maximum(t - GAP, 0), 1, own_w, put_side)

        @pl.when(t < total)
        def _():
            far_copy(t).wait_recv()
            value = near_p[...] + far_in[at(t)].astype(jnp.float32)
            near_out[at(t)] = value.astype(jnp.bfloat16)
            near_copy(t).start()

        @pl.when(t >= GAP)
        def _():
            k = jnp.maximum(t - GAP, 0)
            near_copy(k).wait_recv()
            value = (side_p[...] + near_in[at(k)].astype(jnp.float32)).astype(jnp.bfloat16)

            @pl.when(k < terms)
            def _():
                j = jnp.minimum(k, terms - 1)
                side_out[at(j)] = value
                side_copy(j).start()

            @pl.when(k >= terms)
            def _():
                mix[at(jnp.maximum(k - terms, 0))] = value

        @pl.when(t == total + GAP - 2)
        def _():
            @pl.loop(0, blocks)
            def _(b):
                where = pl.ds(pl.multiple_of(b * block, block), block)
                early[where] = jnp.dot(
                    amp[where, :split], mix[:split], preferred_element_type=jnp.float32
                )

    @pl.loop(0, blocks)
    def _(b):
        for c in range(block // chunk):
            side_copy(b * (block // chunk) + c).wait_recv()
        where = pl.ds(pl.multiple_of(b * block, block), block)
        value = early[where] + side_in[where].astype(jnp.float32)
        value = value + jnp.dot(
            amp[where, split:], mix[split:], preferred_element_type=jnp.float32
        )
        value = jnp.where(alive(b * block, block), value, jnp.zeros_like(value))
        out[0, 0, where] = value.astype(jnp.bfloat16)

    @pl.loop(0, total)
    def _(k):
        far_copy(k).wait_send()
        near_copy(k).wait_send()

    @pl.loop(0, terms)
    def _(k):
        side_copy(k).wait_send()

    @pl.loop(0, mixes)
    def _(m):
        mix_copy(m).wait_send()


def shards(half, amplitudes, live_rows, hole_coupling, part_hole, recoupling):
    rows, holes = amplitudes.shape[2:]
    chunk, block = min(CHUNK, holes), min(BLOCK, rows)
    total = (rows + holes) // chunk
    terms = rows // chunk
    bf = jnp.bfloat16
    stream = pltpu.VMEM((rows + holes, holes), bf)
    sems = pltpu.SemaphoreType.DMA
    flops = 10 * rows * holes * holes
    return pl.pallas_call(
        functools.partial(kernel, half, chunk, block, min(HEAD, block // chunk)),
        out_shape=pltpu.VMEM(amplitudes.shape, bf),
        in_specs=[pl.BlockSpec(memory_space=pltpu.SMEM)] * 2
        + [pl.BlockSpec(memory_space=pl.ANY)] * 3,
        out_specs=pl.BlockSpec(memory_space=pltpu.VMEM),
        scratch_shapes=[
            pltpu.VMEM((rows, holes), bf),
            pltpu.VMEM((3, holes, holes), bf),
            pltpu.VMEM((rows, holes), bf),
            pltpu.VMEM((holes, holes), jnp.float32),
            pltpu.VMEM((holes, holes), bf),
            pltpu.VMEM((holes, holes), bf),
            pltpu.VMEM((holes, holes), bf),
            pltpu.VMEM((rows, holes), jnp.float32),
            stream, stream, stream, stream,
            pltpu.VMEM((rows, holes), bf),
            pltpu.VMEM((rows, holes), bf),
            pltpu.VMEM((chunk, holes), jnp.float32),
            pltpu.VMEM((chunk, holes), jnp.float32),
            sems((rows // block,)),
            sems((rows // block,)),
            sems((3,)),
            sems((total,)), sems((total,)), sems((total,)), sems((total,)),
            sems((terms,)), sems((terms,)),
            sems((holes // chunk,)), sems((holes // chunk,)),
        ],
        compiler_params=pltpu.CompilerParams(
            collective_id=0, has_side_effects=True, vmem_limit_bytes=60 << 20
        ),
        cost_estimate=pl.CostEstimate(
            flops=flops, bytes_accessed=6 * rows * holes * 2, transcendentals=0
        ),
        name="gt_bar",
    )(recoupling.T, live_rows, amplitudes, hole_coupling, part_hole)


def solution(mesh):
    in_specs = (
        P("ja", "pt", None, None),
        P("ja", "pt"),
        P("ja", "pt", None, None, None),
        P("ja", "pt", None, None),
        P(),
    )
    out_specs = P("ja", "pt", None, None)
    body = functools.partial(shards, mesh.shape["ja"] // 2)
    return jax.shard_map(body, mesh=mesh, in_specs=in_specs, out_specs=out_specs, check_vma=False)
```
